768 devices in a mesh: rows: 96 (over z, x, core), grp: 8 (over y).
Axes of the slice: x: 4, y: 8, z: 12, core: 2. Of those that a mesh axis runs over, the one named last changes fastest.
Arguments:
- user_factors: bfloat16 [393216, 512], P(('rows', 'grp')), may hold values from -6 to 6
- item_factors: bfloat16 [2048, 512], P('grp'), may hold values from -0.25 to 0.25
- obs_user: int32 [6144], P(('rows', 'grp')), may hold values from 0 to 3
- obs_item: int32 [6144], P(('rows', 'grp')), may hold values from 0 to 15, as said below
- obs_weight: bfloat16 [6144, 128, 128], P(('rows', 'grp')), may hold values from 0.5 to 8
- obs_target: bfloat16 [6144, 128, 128], P(('rows', 'grp')), may hold values from -6 to 6
Outputs:
- user_grad: float32 [393216, 512], P(('rows', 'grp'))
- item_grad: float32 [2048, 512], P('grp')
The draws below stay inside these ranges and needn't reach their ends.
Inputs may be any that keep to these rules, and one draw needn't show every extreme that they name: `obs_item`: the item tiles of one device's 8 observed tiles are all different.
All inputs are finite; a program needn't handle non-finite values.
Results may differ from the reference program's by a relative error of at most 0.0014.
Values may be sent and summed in bfloat16 or wider, within the bound.
A program may use at most 32 MiB of HBM per device.

```python
import math
import jax
import jax.numpy as jnp
from jax import lax

F = 512
BLOCK = 128
UB_DEV = 4
NB_DEV = 8
USERS = 393216
ITEM_BLOCKS = 16
ITEMS = 2048
OBS = 6144


def draw_obs_item(key, part):
    device_keys = jax.random.split(key, OBS // NB_DEV)
    picks = jax.vmap(lambda one_key: jax.random.permutation(one_key, ITEM_BLOCKS)[:NB_DEV])(device_keys)
    return picks.reshape(OBS).astype(jnp.int32)


def touch_ends(drawn, rng, smallest, high):
    longest = drawn.shape.index(max(drawn.shape))
    spots = []
    for shift in (0, 1):
        where = [jax.random.randint(jax.random.fold_in(rng, axis), (), 0, length) for axis, length in enumerate(drawn.shape)]
        where[longest] = (where[longest] + shift) % drawn.shape[longest]
        spots.append(tuple(where))
    return drawn.at[spots[0]].set(smallest).at[spots[1]].set(high)


def levels(rng, shape, pieces, low, top_value):
    level, own = 1.0, jax.random.fold_in(rng, 6)
    for position, parts in pieces:
        draws = jnp.exp(jax.random.uniform(jax.random.fold_in(own, position), (parts,), jnp.float32, low / len(pieces), top_value / len(pieces)))
        level = level * jnp.repeat(draws, shape[position] // parts).reshape([-1 if axis == position else 1 for axis in range(len(shape))])
    return level


def normal_values(own_key, extent, width, most, pieces=(), kind=jnp.bfloat16):
    level = levels(own_key, extent, pieces, -0.22, 0.18) if pieces else 1.0
    result = jax.random.normal(own_key, extent, jnp.float32) * width * level
    return jnp.minimum(jnp.maximum(result, -most), most).astype(kind)


def setup_inputs(seed: int = 0) -> dict:
    splits = jax.random.split(jax.random.key(seed), 7)
    user_factors = normal_values(splits[0], (USERS, F), 1.0, 6.0, ((0, 768),))
    item_factors = normal_values(splits[1], (ITEMS, F), F ** -0.5, 0.25, ((0, 8),))
    obs_user = touch_ends(jax.random.randint(splits[2], (OBS,), 0, UB_DEV), jax.random.fold_in(splits[2], 1), 0, UB_DEV - 1).astype(jnp.int32)
    obs_item = draw_obs_item(jax.random.fold_in(splits[6], 71), 0)
    obs_weight = jnp.clip(jnp.exp(math.log(8.0) - 2.7725887 * jax.random.uniform(splits[4], (OBS, BLOCK, BLOCK), jnp.float32) ** levels(splits[4], (OBS, BLOCK, BLOCK), ((0, 768),), -0.2, 0.2)), 0.5, 8.0).astype(jnp.bfloat16)
    obs_target = normal_values(splits[5], (OBS, BLOCK, BLOCK), 1.0, 6.0, ((0, 768),))
    return dict(user_factors=user_factors, item_factors=item_factors, obs_user=obs_user, obs_item=obs_item, obs_weight=obs_weight, obs_target=obs_target)


def reference(user_factors, item_factors, obs_user, obs_item, obs_weight, obs_target):
    device_count = obs_user.shape[0] // NB_DEV
    item_tiles = item_factors.reshape(ITEM_BLOCKS, BLOCK, F)
    user_tiles = user_factors.reshape(device_count, UB_DEV, BLOCK, F)
    inputs_all = (user_tiles,
                  obs_user.reshape(device_count, NB_DEV),
                  obs_item.reshape(device_count, NB_DEV),
                  obs_weight.reshape(device_count, NB_DEV, BLOCK, BLOCK),
                  obs_target.reshape(device_count, NB_DEV, BLOCK, BLOCK))

    def one_device(running, inputs_one):
        user_rows, which_user, which_item, weights, targets = inputs_one
        user_picked = user_rows[which_user].astype(jnp.float32)
        item_picked = item_tiles[which_item].astype(jnp.float32)
        predicted = jnp.einsum("kuf,kif->kui", user_picked, item_picked)
        residual = (weights.astype(jnp.float32) * (predicted - targets.astype(jnp.float32)) / 16.0).astype(jnp.bfloat16)
        residual_wide = residual.astype(jnp.float32)
        item_terms = jnp.einsum("kui,kuf->kif", residual_wide, user_picked).astype(jnp.bfloat16)
        running = running.at[which_item].add(item_terms.astype(jnp.float32))
        user_part = jnp.einsum("kui,kif->kuf", residual_wide, item_picked)
        user_terms = jnp.zeros((UB_DEV, BLOCK, F), jnp.float32).at[which_user].add(user_part)
        return running, user_terms

    item_sum, user_terms = lax.scan(one_device, jnp.zeros((ITEM_BLOCKS, BLOCK, F), jnp.float32), inputs_all)
    user_terms = user_terms.reshape(USERS, F)
    gram_items = jnp.dot(item_factors.T, item_factors, preferred_element_type=jnp.float32)
    user_wide = user_factors.astype(jnp.float32)
    user_grad = user_terms + 0.05 * jnp.dot(user_wide, gram_items, precision=lax.Precision.HIGHEST) + 0.1 * user_wide
    item_wide = item_factors.astype(jnp.float32)
    item_grad = item_sum.reshape(ITEMS, F) / 32.0 + 0.1 * item_wide
    return user_grad, item_grad
```

```python
import jax
import jax.numpy as jnp
from jax import lax
from jax.experimental import pallas as pl
from jax.experimental.pallas import tpu as pltpu
from jax.sharding import PartitionSpec as P

MESH = pl.DeviceIdType.MESH
NX, NY, NZ = 4, 8, 12
STEPS = [0, -1, 1, -2, 2, -3, 3, 4]
F32 = jnp.float32
BF16 = jnp.bfloat16


def dot(a, b, ca, cb):
    return lax.dot_general(a, b, (((ca,), (cb,)), ((), ())), preferred_element_type=F32)


def kernel(
    obs_user, obs_item, u_hbm, v_hbm, w_hbm, t_hbm, ug_hbm, is_hbm,
    uv, vt, wv, tv, tb, xr, ys, yr, q, zr, z1, tr, ob, rm, gh, ug,
    sem_in, sem_out, ag_s, ag_r, sb_s, sb_r, x_s, x_r, y_s, y_r, z_s, z_r, g_s, g_r,
):
    r = lax.axis_index("rows")
    y = lax.axis_index("grp")
    c = lax.rem(r, 2)
    x = lax.rem(r // 2, NX)
    z = r // (2 * NX)
    i, g = lax.rem(z, 4), z // 4

    def dev(dx=0, dy=0, di=0, dg=0, dc=0):
        cc = 1 - c if dc else c
        xx = lax.rem(x + dx, NX)
        zz = lax.rem(g + dg, 3) * 4 + lax.rem(i + di, 4)
        return ((zz * NX + xx) * 2 + cc, lax.rem(y + dy + NY, NY))

    def yat(d):
        return lax.rem(y + STEPS[d] + NY, NY)

    def remote(src, dst, s, t, to):
        return pltpu.make_async_remote_copy(src, dst, s, t, device_id=to, device_id_type=MESH)

    loads = [
        pltpu.make_async_copy(v_hbm, vt.at[pl.ds(2 * y, 2)], sem_in.at[0]),
        pltpu.make_async_copy(u_hbm, uv, sem_in.at[1]),
        pltpu.make_async_copy(w_hbm, wv, sem_in.at[2]),
        pltpu.make_async_copy(t_hbm, tv, sem_in.at[3]),
    ]
    for cp in loads:
        cp.start()

    peers = [dev(dy=d) for d in range(1, NY)]
    peers += [dev(dx=dx, dc=dc) for dx in range(NX) for dc in range(2) if dx or dc]
    peers += [dev(di=d) for d in range(1, 4)] + [dev(dg=d) for d in range(1, 3)]
    barrier = pltpu.get_barrier_semaphore()
    for p in peers:
        pl.semaphore_signal(barrier, inc=1, device_id=p, device_id_type=MESH)
    for cp in loads:
        cp.wait()
    pl.semaphore_wait(barrier, len(peers))

    pending = []

    def ag(direction, step, h):
        sgn = 1 if direction == 0 else -1
        src_y = lax.rem(y - sgn * (step - 1) + NY, NY)
        ref = vt.at[2 * src_y + c, h]
        k = (direction * 4 + step - 1) * 2 + h
        return remote(ref, ref, ag_s.at[k], ag_r.at[k], dev(dy=sgn))

    def ag_has(direction, step, h):
        return step < 4 or h == direction

    def to_sibling(d, h):
        ref = vt.at[2 * yat(d) + c, h]
        return remote(ref, ref, sb_s.at[d * 2 + h], sb_r.at[d * 2 + h], dev(dc=1))

    def tile(d, dc):
        yy = yat(d)
        cc = 1 - c if dc else c
        b = 2 * yy + cc
        k = jnp.int32(0)
        scale = F32(0.0)
        for n in range(8):
            hit = obs_item[n] == b
            k = jnp.where(hit, n, k)
            scale = jnp.where(hit, F32(0.0625), scale)
        j = obs_user[k]
        uk = uv[j]
        vb = vt[b].reshape(128, 512)
        predicted = dot(uk, vb, 1, 1)
        res = (wv[k].astype(F32) * (predicted - tv[k].astype(F32)) * scale).astype(BF16)
        tb[d, dc] = dot(res, uk, 0, 0).astype(BF16).reshape(4, 32, 512)
        for jj in range(4):
            keep = jnp.where(j == jj, F32(1.0), F32(0.0)).astype(BF16)
            rm[b, jj] = res * keep
        for dx in range(NX):
            if dx or dc:
                e = dx * 2 + dc
                cp = remote(
                    tb.at[d, dc, lax.rem(x + dx, NX)], xr.at[d, e],
                    x_s.at[d * 8 + e], x_r.at[d * 8 + e], dev(dx=dx, dc=dc),
                )
                cp.start()
                pending.append(cp)

    def reduce_x(d):
        total = tb[d, 0, x].astype(F32)
        for e in range(1, 8):
            remote(xr.at[d, e], xr.at[d, e], x_s.at[d * 8 + e], x_r.at[d * 8 + e], dev(dc=1)).wait_recv()
            total = total + xr[d, e].astype(F32)
        if d == 0:
            yr[0] = total
        else:
            ys[d] = total
            cp = remote(ys.at[d], yr.at[d], y_s.at[d], y_r.at[d], dev(dy=STEPS[d]))
            cp.start()
            pending.append(cp)

    for direction in range(2):
        for h in range(2):
            cp = ag(direction, 1, h)
            cp.start()
            pending.append(cp)
    tile(0, 0)
    tile(0, 1)
    for step in range(1, 5):
        here = [2 * step - 1, 2 * step] if step < 4 else [7, 7]
        for h in range(2):
            for direction in range(2):
                if not ag_has(direction, step, h):
                    continue
                ag(direction, step, h).wait_recv()
                if step < 4 and ag_has(direction, step + 1, h):
                    cp = ag(direction, step + 1, h)
                    cp.start()
                    pending.append(cp)
                cp = to_sibling(here[direction], h)
                cp.start()
                pending.append(cp)
        ds = here if step < 4 else [7]
        for d in ds:
            tile(d, 0)
        for d in ds:
            for h in range(2):
                to_sibling(d, h).wait_recv()
            tile(d, 1)
        if step == 1:
            reduce_x(0)
        else:
            for d in [2 * step - 3, 2 * step - 2]:
                reduce_x(d)
    reduce_x(7)

    table = vt[...].reshape(2048, 512)
    gram = 0.05 * dot(table, table, 0, 0)
    hi = gram.astype(BF16)
    gh[0] = hi
    rest = gram - hi.astype(F32)
    mid = rest.astype(BF16)
    gh[1] = mid
    gh[2] = (rest - mid.astype(F32)).astype(BF16)

    total = yr[0]
    for d in range(1, 8):
        remote(yr.at[d], yr.at[d], y_s.at[d], y_r.at[d], dev(dc=1)).wait_recv()
        total = total + yr[d]
    q[...] = total.reshape(4, 8, 512)
    for d in range(1, 4):
        cp = remote(q.at[lax.rem(i + d, 4)], zr.at[d], z_s.at[d], z_r.at[d], dev(di=d))
        cp.start()
        pending.append(cp)

    def user(j):
        uj = uv[j]
        acc = 0.1 * uj.astype(F32)
        for n in range(3):
            acc = acc + dot(uj, gh[n], 1, 0)
        for b in range(16):
            acc = acc + dot(rm[b, j], vt[b].reshape(128, 512), 1, 0)
        ug[j] = acc
        cp = pltpu.make_async_copy(ug.at[j], ug_hbm.at[j], sem_out.at[j])
        cp.start()
        return cp

    outs = [user(0), user(1)]

    total = q[i]
    for d in range(1, 4):
        remote(zr.at[d], zr.at[d], z_s.at[d], z_r.at[d], dev(dc=1)).wait_recv()
        total = total + zr[d]
    z1[...] = total
    for d in range(1, 3):
        cp = remote(z1, tr.at[g], z_s.at[3 + d], z_r.at[3 + d], dev(dg=d))
        cp.start()
        pending.append(cp)
    tr[g] = total
    outs += [user(2), user(3)]
    for d in range(1, 3):
        remote(z1, z1, z_s.at[3 + d], z_r.at[3 + d], dev(dc=1)).wait_recv()
    ob[c, x, i] = tr[0] + tr[1] + tr[2]

    def spread(ref, k, to):
        return remote(ref, ref, g_s.at[k], g_r.at[k], to)

    for d in range(1, 4):
        cp = spread(ob.at[c, x, i], d, dev(di=d))
        cp.start()
        pending.append(cp)
    for d in range(1, 4):
        spread(ob.at[c, x, i], d, dev(di=d)).wait_recv()
    for d in range(1, 4):
        cp = spread(ob.at[c, x], 4 + d, dev(dx=d))
        cp.start()
        pending.append(cp)
    cp = spread(ob.at[c, x], 8, dev(dc=1))
    cp.start()
    pending.append(cp)
    for d in range(1, 4):
        ref = ob.at[c, lax.rem(x + NX - d, NX)]
        spread(ref, 4 + d, dev(dx=d)).wait_recv()
        cp = spread(ref, 8 + d, dev(dc=1))
        cp.start()
        pending.append(cp)
    for d in range(4):
        spread(ob.at[c, x], 8 + d, dev(dc=1)).wait_recv()
    cp = pltpu.make_async_copy(ob, is_hbm, sem_out.at[4])
    cp.start()
    outs.append(cp)
    for cp in pending:
        cp.wait_send()
    for cp in outs:
        cp.wait()


def local(user_factors, item_factors, obs_user, obs_item, obs_weight, obs_target):
    anyspace = pl.BlockSpec(memory_space=pl.ANY)
    smem = pl.BlockSpec(memory_space=pltpu.SMEM)
    dma = pltpu.SemaphoreType.DMA
    user_grad, item_sum = pl.pallas_call(
        kernel,
        out_shape=(
            jax.ShapeDtypeStruct((4, 128, 512), F32),
            jax.ShapeDtypeStruct((2, 4, 4, 8, 512), F32),
        ),
        in_specs=[smem, smem, anyspace, anyspace, anyspace, anyspace],
        out_specs=(anyspace, anyspace),
        scratch_shapes=[
            pltpu.VMEM((4, 128, 512), BF16),
            pltpu.VMEM((16, 2, 64, 512), BF16),
            pltpu.VMEM((8, 128, 128), BF16),
            pltpu.VMEM((8, 128, 128), BF16),
            pltpu.VMEM((8, 2, 4, 32, 512), BF16),
            pltpu.VMEM((8, 8, 32, 512), BF16),
            pltpu.VMEM((8, 32, 512), F32),
            pltpu.VMEM((8, 32, 512), F32),
            pltpu.VMEM((4, 8, 512), F32),
            pltpu.VMEM((4, 8, 512), F32),
            pltpu.VMEM((8, 512), F32),
            pltpu.VMEM((3, 8, 512), F32),
            pltpu.VMEM((2, 4, 4, 8, 512), F32),
            pltpu.VMEM((16, 4, 128, 128), BF16),
            pltpu.VMEM((3, 512, 512), BF16),
            pltpu.VMEM((4, 128, 512), F32),
            dma((4,)), dma((5,)),
            dma((16,)), dma((16,)),
            dma((16,)), dma((16,)),
            dma((64,)), dma((64,)),
            dma((8,)), dma((8,)),
            dma((8,)), dma((8,)),
            dma((16,)), dma((16,)),
        ],
        compiler_params=pltpu.CompilerParams(
            collective_id=0, has_side_effects=True, vmem_limit_bytes=48 << 20
        ),
    )(
        obs_user,
        obs_item,
        user_factors.reshape(4, 128, 512),
        item_factors.reshape(2, 2, 64, 512),
        obs_weight,
        obs_target,
    )
    item_grad = item_sum.reshape(256, 512) / 32.0 + 0.1 * item_factors.astype(F32)
    return user_grad.reshape(512, 512), item_grad


def solution(mesh):
    both = P(("rows", "grp"))
    placed = (
        P(("rows", "grp"), None),
        P("grp", None),
        both,
        both,
        P(("rows", "grp"), None, None),
        P(("rows", "grp"), None, None),
    )
    return jax.shard_map(
        local,
        mesh=mesh,
        in_specs=placed,
        out_specs=(P(("rows", "grp"), None), P("grp", None)),
        check_vma=False,
    )
```

```python
import jax
import jax.numpy as jnp
from jax import lax
from jax.experimental import pallas as pl
from jax.experimental.pallas import tpu as pltpu
from jax.sharding import PartitionSpec as P

MESH = pl.DeviceIdType.MESH
NX, NY = 4, 8
STEPS = [0, -1, 1, -2, 2, -3, 3, 4]
GROUPS = [[0], [1, 2], [3, 4], [5, 6], [7]]
VMEM = 56 << 20
FULL_BARRIER = 0
F32 = jnp.float32
BF16 = jnp.bfloat16


def dot(a, b, ca, cb):
    return lax.dot_general(a, b, (((ca,), (cb,)), ((), ())), preferred_element_type=F32)


def kernel(
    obs_user, obs_item, u_hbm, v_hbm, w_hbm, t_hbm, ug_hbm, ig_hbm,
    uv, vt, wv, tv, ta, tb, xa, xb, ys, yr, qa, qb, za, zb, z1, tr, ob, rm, gh, ug, ig,
    sem_in, sem_out, ag_s, ag_r, sb_s, sb_r, xa_s, xa_r, xb_s, xb_r,
    y_s, y_r, z_s, z_r, g_s, g_r,
):
    r = lax.axis_index("rows")
    y = lax.axis_index("grp")
    c = lax.rem(r, 2)
    x = lax.rem(r // 2, NX)
    z = r // (2 * NX)
    i, g = lax.rem(z, 4), z // 4

    def dev(dx=0, dy=0, di=0, dg=0, dc=0):
        cc = 1 - c if dc else c
        xx = lax.rem(x + dx, NX) if dx else x
        yy = lax.rem(y + dy + NY, NY) if dy else y
        gg = lax.rem(g + dg, 3) if dg else g
        zz = gg * 4 + (lax.rem(i + di, 4) if di else i)
        return ((zz * NX + xx) * 2 + cc, yy)

    def yat(d):
        return lax.rem(y + STEPS[d] + NY, NY)

    def remote(src, dst, s, t, to):
        return pltpu.make_async_remote_copy(src, dst, s, t, device_id=to, device_id_type=MESH)

    pending = []
    outs = []

    def send(cp):
        cp.start()
        pending.append(cp)

    loads = [
        pltpu.make_async_copy(v_hbm, vt.at[pl.ds(2 * y, 2)], sem_in.at[0]),
        pltpu.make_async_copy(u_hbm, uv, sem_in.at[1]),
        pltpu.make_async_copy(w_hbm, wv, sem_in.at[2]),
        pltpu.make_async_copy(t_hbm, tv, sem_in.at[3]),
    ]
    for cp in loads:
        cp.start()

    peers = [dev(dy=1), dev(dy=-1), dev(dc=1)]
    peers += [dev(dx=d, dc=dc) for d in range(1, 4) for dc in range(2)]
    peers += [dev(di=d, dc=dc) for d in range(1, 4) for dc in range(2)]
    peers += [dev(dg=1), dev(dg=2)]
    if FULL_BARRIER:
        peers += [dev(dy=d) for d in range(2, 7)]
        peers += [dev(dx=dx, di=di) for dx in range(1, 4) for di in range(1, 4)]
    barrier = pltpu.get_barrier_semaphore()
    for p in peers:
        pl.semaphore_signal(barrier, inc=1, device_id=p, device_id_type=MESH)
    for cp in loads:
        cp.wait()
    pl.semaphore_wait(barrier, len(peers))

    def ag(direction, step, h):
        sgn = 1 if direction == 0 else -1
        src_y = lax.rem(y - sgn * (step - 1) + NY, NY)
        ref = vt.at[2 * src_y + c, h]
        k = (direction * 4 + step - 1) * 2 + h
        return remote(ref, ref, ag_s.at[k], ag_r.at[k], dev(dy=sgn))

    def ag_has(direction, step, h):
        return step < 4 or h == direction

    def to_sibling(d, h):
        ref = vt.at[2 * yat(d) + c, h]
        return remote(ref, ref, sb_s.at[2 * d + h], sb_r.at[2 * d + h], dev(dc=1))

    def tile(d, dc):
        yy = yat(d)
        cc = 1 - c if dc else c
        b = 2 * yy + cc
        k = jnp.int32(0)
        scale = F32(0.0)
        for n in range(8):
            hit = obs_item[n] == b
            k = jnp.where(hit, n, k)
            scale = jnp.where(hit, F32(0.0625), scale)
        j = obs_user[k]
        uk = uv[j]
        vb = vt[b].reshape(128, 512)
        predicted = dot(uk, vb, 1, 1)
        res = (wv[k].astype(F32) * (predicted - tv[k].astype(F32)) * scale).astype(BF16)
        term = dot(res, uk, 0, 0)
        for n in range(4):
            ta[d, dc, n] = term[24 * n : 24 * n + 24].astype(BF16)
            tb[d, dc, n] = term[96 + 8 * n : 104 + 8 * n].astype(BF16)
        for jj in range(4):
            keep = jnp.where(j == jj, F32(1.0), F32(0.0)).astype(BF16)
            rm[b, jj] = res * keep

    def terms(grp, dc):
        ds = GROUPS[grp]
        dd = pl.ds(ds[0], len(ds))
        for n in range(NX):
            if n or dc:
                e = n * 2 + dc
                k = grp * 8 + e
                xx = lax.rem(x + n, NX)
                ii = lax.rem(i + n, 4)
                send(remote(ta.at[dd, dc, xx], xa.at[dd, e], xa_s.at[k], xa_r.at[k], dev(dx=n, dc=dc)))
                send(remote(tb.at[dd, dc, ii], xb.at[dd, e], xb_s.at[k], xb_r.at[k], dev(di=n, dc=dc)))

    def reduce_group(grp):
        ds = GROUPS[grp]
        dd = pl.ds(ds[0], len(ds))
        for e in range(1, 8):
            k = grp * 8 + e
            remote(xa.at[dd, e], xa.at[dd, e], xa_s.at[k], xa_r.at[k], dev(dc=1)).wait_recv()
            remote(xb.at[dd, e], xb.at[dd, e], xb_s.at[k], xb_r.at[k], dev(dc=1)).wait_recv()
        for d in ds:
            sa = ta[d, 0, x].astype(F32)
            sb = tb[d, 0, i].astype(F32)
            for e in range(1, 8):
                sa = sa + xa[d, e].astype(F32)
                sb = sb + xb[d, e].astype(F32)
            dst = ys if d else yr
            dst[d, 0:24] = sa
            dst[d, 24:32] = sb
            if d:
                send(remote(ys.at[d], yr.at[d], y_s.at[d], y_r.at[d], dev(dy=STEPS[d])))

    def arrive(step, h):
        for direction in range(2):
            if ag_has(direction, step, h):
                ag(direction, step, h).wait_recv()
                if step < 4 and ag_has(direction, step + 1, h):
                    send(ag(direction, step + 1, h))
                send(to_sibling(GROUPS[step][direction] if step < 4 else 7, h))

    def other(d):
        for h in range(2):
            to_sibling(d, h).wait_recv()
        tile(d, 1)

    for h in range(2):
        for direction in range(2):
            send(ag(direction, 1, h))
    tile(0, 1)
    terms(0, 1)
    tile(0, 0)
    terms(0, 0)
    arrive(1, 0)
    arrive(1, 1)
    for step in range(1, 4):
        low, high = GROUPS[step]
        tile(low, 0)
        arrive(step + 1, 0)
        tile(high, 0)
        terms(step, 0)
        arrive(step + 1, 1)
        other(low)
        other(high)
        terms(step, 1)
        reduce_group(step - 1)
    tile(7, 0)
    terms(4, 0)
    other(7)
    terms(4, 1)
    reduce_group(3)
    reduce_group(4)

    table = vt[...].reshape(2048, 512)
    gram = 0.05 * dot(table, table, 0, 0)
    hi = gram.astype(BF16)
    gh[0] = hi
    rest = gram - hi.astype(F32)
    mid = rest.astype(BF16)
    gh[1] = mid
    gh[2] = (rest - mid.astype(F32)).astype(BF16)

    total = yr[0]
    for d in range(1, 8):
        remote(yr.at[d], yr.at[d], y_s.at[d], y_r.at[d], dev(dc=1)).wait_recv()
        total = total + yr[d]
    for n in range(4):
        qa[n] = total[0:24, 128 * n : 128 * n + 128]
        qb[n] = total[24:32, 128 * n : 128 * n + 128]
    for d in range(1, 4):
        send(remote(qa.at[lax.rem(i + d, 4)], za.at[d], z_s.at[d], z_r.at[d], dev(di=d)))
        send(remote(qb.at[lax.rem(x + d, 4)], zb.at[d], z_s.at[4 + d], z_r.at[4 + d], dev(dx=d)))

    def user(j):
        uj = uv[j]
        acc = 0.1 * uj.astype(F32)
        for n in range(3):
            acc = acc + dot(uj, gh[n], 1, 0)
        for b in range(16):
            acc = acc + dot(rm[b, j], vt[b].reshape(128, 512), 1, 0)
        ug[j] = acc
        cp = pltpu.make_async_copy(ug.at[j], ug_hbm.at[j], sem_out.at[j])
        cp.start()
        outs.append(cp)

    user(0)
    user(1)

    pa, pb = qa[i], qb[x]
    for d in range(1, 4):
        remote(za.at[d], za.at[d], z_s.at[d], z_r.at[d], dev(dc=1)).wait_recv()
        remote(zb.at[d], zb.at[d], z_s.at[4 + d], z_r.at[4 + d], dev(dc=1)).wait_recv()
        pa = pa + za[d]
        pb = pb + zb[d]
    z1[0:24] = pa
    z1[24:32] = pb
    for d in range(1, 3):
        send(remote(z1, tr.at[g], z_s.at[8 + d], z_r.at[8 + d], dev(dg=d)))
    tr[g] = z1[...]
    user(2)
    user(3)
    for d in range(1, 3):
        remote(z1, z1, z_s.at[8 + d], z_r.at[8 + d], dev(dc=1)).wait_recv()
    ob[c, x, i] = tr[0] + tr[1] + tr[2]

    def spread(ref, k, to):
        return remote(ref, ref, g_s.at[k], g_r.at[k], to)

    for dx in range(NX):
        for di in range(4):
            if dx or di:
                send(spread(ob.at[c, x, i], dx * 4 + di, dev(dx=dx, di=di)))
    for dx in range(NX):
        for di in range(4):
            if dx or di:
                spread(ob.at[c, x, i], dx * 4 + di, dev(dx=dx, di=di)).wait_recv()
        send(spread(ob.at[c, lax.rem(x + NX - dx, NX)], 16 + dx, dev(dc=1)))
    for dx in range(NX):
        spread(ob.at[c, x], 16 + dx, dev(dc=1)).wait_recv()
    own = vt[pl.ds(2 * y, 2)].reshape(256, 512)
    for cc in range(2):
        for xx in range(NX):
            for ii in range(4):
                lo = cc * 128 + 24 * xx
                ig[lo : lo + 24, 128 * ii : 128 * ii + 128] = ob[cc, xx, ii, 0:24]
                lo = cc * 128 + 96 + 8 * ii
                ig[lo : lo + 8, 128 * xx : 128 * xx + 128] = ob[cc, xx, ii, 24:32]
    ig[...] = ig[...] * (1.0 / 32.0) + 0.1 * own.astype(F32)
    cp = pltpu.make_async_copy(ig, ig_hbm, sem_out.at[4])
    cp.start()
    outs.append(cp)
    for cp in pending:
        cp.wait_send()
    for cp in outs:
        cp.wait()


def place(ug, ig, ug_out, ig_out, uv, iv, sem):
    parts = [(ug.at[j], uv.at[j], ug_out.at[j]) for j in range(4)] + [(ig, iv, ig_out)]
    fetch = [pltpu.make_async_copy(p[0], p[1], sem.at[0, n]) for n, p in enumerate(parts)]
    store = [pltpu.make_async_copy(p[1], p[2], sem.at[1, n]) for n, p in enumerate(parts)]
    for cp in fetch:
        cp.start()
    for f, t in zip(fetch, store):
        f.wait()
        t.start()
    for cp in store:
        cp.wait()


def local(user_factors, item_factors, obs_user, obs_item, obs_weight, obs_target):
    hbm = pl.BlockSpec(memory_space=pltpu.HBM)
    smem = pl.BlockSpec(memory_space=pltpu.SMEM)
    dma = pltpu.SemaphoreType.DMA
    shapes = (
        jax.ShapeDtypeStruct((4, 128, 512), F32),
        jax.ShapeDtypeStruct((256, 512), F32),
    )
    made = pl.pallas_call(
        kernel,
        out_shape=shapes,
        in_specs=[smem, smem, hbm, hbm, hbm, hbm],
        out_specs=(hbm, hbm),
        scratch_shapes=[
            pltpu.VMEM((4, 128, 512), BF16),
            pltpu.VMEM((16, 2, 64, 512), BF16),
            pltpu.VMEM((8, 128, 128), BF16),
            pltpu.VMEM((8, 128, 128), BF16),
            pltpu.VMEM((8, 2, 4, 24, 512), BF16),
            pltpu.VMEM((8, 2, 4, 8, 512), BF16),
            pltpu.VMEM((8, 8, 24, 512), BF16),
            pltpu.VMEM((8, 8, 8, 512), BF16),
            pltpu.VMEM((8, 32, 512), F32),
            pltpu.VMEM((8, 32, 512), F32),
            pltpu.VMEM((4, 24, 128), F32),
            pltpu.VMEM((4, 8, 128), F32),
            pltpu.VMEM((4, 24, 128), F32),
            pltpu.VMEM((4, 8, 128), F32),
            pltpu.VMEM((32, 128), F32),
            pltpu.VMEM((3, 32, 128), F32),
            pltpu.VMEM((2, 4, 4, 32, 128), F32),
            pltpu.VMEM((16, 4, 128, 128), BF16),
            pltpu.VMEM((3, 512, 512), BF16),
            pltpu.VMEM((4, 128, 512), F32),
            pltpu.VMEM((256, 512), F32),
            dma((4,)), dma((5,)),
            dma((16,)), dma((16,)),
            dma((16,)), dma((16,)),
            dma((40,)), dma((40,)),
            dma((40,)), dma((40,)),
            dma((8,)), dma((8,)),
            dma((12,)), dma((12,)),
            dma((20,)), dma((20,)),
        ],
        compiler_params=pltpu.CompilerParams(
            collective_id=0, has_side_effects=True, vmem_limit_bytes=VMEM
        ),
    )(
        obs_user,
        obs_item,
        user_factors.reshape(4, 128, 512),
        item_factors.reshape(2, 2, 64, 512),
        obs_weight,
        obs_target,
    )
    user_grad, item_grad = pl.pallas_call(
        place,
        out_shape=shapes,
        in_specs=[hbm, hbm],
        out_specs=(hbm, hbm),
        scratch_shapes=[pltpu.VMEM((4, 128, 512), F32), pltpu.VMEM((256, 512), F32), dma((2, 5))],
        compiler_params=pltpu.CompilerParams(vmem_limit_bytes=VMEM),
    )(*made)
    return user_grad.reshape(512, 512), item_grad


def solution(mesh):
    both = P(("rows", "grp"))
    placed = (
        P(("rows", "grp"), None),
        P("grp", None),
        both,
        both,
        P(("rows", "grp"), None, None),
        P(("rows", "grp"), None, None),
    )
    return jax.shard_map(
        local,
        mesh=mesh,
        in_specs=placed,
        out_specs=(P(("rows", "grp"), None), P("grp", None)),
        check_vma=False,
    )
```

```python
import jax
import jax.numpy as jnp
from jax import lax
from jax.experimental import pallas as pl
from jax.experimental.pallas import tpu as pltpu
from jax.sharding import PartitionSpec as P

MESH = pl.DeviceIdType.MESH
NX, NY = 4, 8
STEPS = [0, -1, 1, -2, 2, -3, 3, 4]
GROUPS = [[0], [1, 2], [3, 4], [5, 6], [7]]
VMEM = 56 << 20
FULL_BARRIER = 0
F32 = jnp.float32
BF16 = jnp.bfloat16


def dot(a, b, ca, cb):
    return lax.dot_general(a, b, (((ca,), (cb,)), ((), ())), preferred_element_type=F32)


def kernel(
    obs_user, obs_item, u_hbm, v_hbm, w_hbm, t_hbm, ug, ig,
    uv, vt, wv, tv, ta, tb, xa, xb, ys, yr, qa, qb, za, zb, z1, tr, ob, rm, gh,
    sem_in, ag_s, ag_r, sb_s, sb_r, xa_s, xa_r, xb_s, xb_r,
    y_s, y_r, z_s, z_r, g_s, g_r,
):
    r = lax.axis_index("rows")
    y = lax.axis_index("grp")
    c = lax.rem(r, 2)
    x = lax.rem(r // 2, NX)
    z = r // (2 * NX)
    i, g = lax.rem(z, 4), z // 4

    def dev(dx=0, dy=0, di=0, dg=0, dc=0):
        cc = 1 - c if dc else c
        xx = lax.rem(x + dx, NX) if dx else x
        yy = lax.rem(y + dy + NY, NY) if dy else y
        gg = lax.rem(g + dg, 3) if dg else g
        zz = gg * 4 + (lax.rem(i + di, 4) if di else i)
        return ((zz * NX + xx) * 2 + cc, yy)

    def yat(d):
        return lax.rem(y + STEPS[d] + NY, NY)

    def remote(src, dst, s, t, to):
        return pltpu.make_async_remote_copy(src, dst, s, t, device_id=to, device_id_type=MESH)

    pending = []

    def drain(keep=0):
        while len(pending) > keep:
            pending.pop(0).wait_send()

    def send(cp):
        cp.start()
        pending.append(cp)

    loads = [
        pltpu.make_async_copy(v_hbm, vt.at[pl.ds(2 * y, 2)], sem_in.at[0]),
        pltpu.make_async_copy(u_hbm, uv, sem_in.at[1]),
        pltpu.make_async_copy(w_hbm, wv, sem_in.at[2]),
        pltpu.make_async_copy(t_hbm, tv, sem_in.at[3]),
    ]
    for cp in loads:
        cp.start()

    peers = [dev(dy=1), dev(dy=-1), dev(dc=1)]
    peers += [dev(dx=d, dc=dc) for d in range(1, 4) for dc in range(2)]
    peers += [dev(di=d, dc=dc) for d in range(1, 4) for dc in range(2)]
    peers += [dev(dg=1), dev(dg=2)]
    if FULL_BARRIER:
        peers += [dev(dy=d) for d in range(2, 7)]
        peers += [dev(dx=dx, di=di) for dx in range(1, 4) for di in range(1, 4)]
    barrier = pltpu.get_barrier_semaphore()
    for p in peers:
        pl.semaphore_signal(barrier, inc=1, device_id=p, device_id_type=MESH)
    for cp in loads:
        cp.wait()
    pl.semaphore_wait(barrier, len(peers))

    def ag(direction, step, h):
        sgn = 1 if direction == 0 else -1
        src_y = lax.rem(y - sgn * (step - 1) + NY, NY)
        ref = vt.at[2 * src_y + c, h]
        k = (direction * 4 + step - 1) * 2 + h
        return remote(ref, ref, ag_s.at[k], ag_r.at[k], dev(dy=sgn))

    def ag_has(direction, step, h):
        return step < 4 or h == direction

    def to_sibling(d, h):
        ref = vt.at[2 * yat(d) + c, h]
        return remote(ref, ref, sb_s.at[2 * d + h], sb_r.at[2 * d + h], dev(dc=1))

    def tile(d, dc):
        yy = yat(d)
        cc = 1 - c if dc else c
        b = 2 * yy + cc
        k = jnp.int32(0)
        scale = F32(0.0)
        for n in range(8):
            hit = obs_item[n] == b
            k = jnp.where(hit, n, k)
            scale = jnp.where(hit, F32(0.0625), scale)
        j = obs_user[k]
        uk = uv[j]
        vb = vt[b].reshape(128, 512)
        predicted = dot(uk, vb, 1, 1)
        res = (wv[k].astype(F32) * (predicted - tv[k].astype(F32)) * scale).astype(BF16)
        term = dot(res, uk, 0, 0)
        for n in range(4):
            ta[d, dc, n] = term[24 * n : 24 * n + 24].astype(BF16)
            tb[d, dc, n] = term[96 + 8 * n : 104 + 8 * n].astype(BF16)
        for jj in range(4):
            keep = jnp.where(j == jj, F32(1.0), F32(0.0)).astype(BF16)
            rm[b, jj] = res * keep

    def terms(grp, dc):
        ds = GROUPS[grp]
        dd = pl.ds(ds[0], len(ds))
        for n in (2, 1, 3, 0):
            if n or dc:
                e = n * 2 + dc
                k = grp * 8 + e
                xx = lax.rem(x + n, NX)
                ii = lax.rem(i + n, 4)
                send(remote(ta.at[dd, dc, xx], xa.at[dd, e], xa_s.at[k], xa_r.at[k], dev(dx=n, dc=dc)))
                send(remote(tb.at[dd, dc, ii], xb.at[dd, e], xb_s.at[k], xb_r.at[k], dev(di=n, dc=dc)))

    def reduce_group(grp):
        ds = GROUPS[grp]
        dd = pl.ds(ds[0], len(ds))
        for e in range(1, 8):
            k = grp * 8 + e
            remote(xa.at[dd, e], xa.at[dd, e], xa_s.at[k], xa_r.at[k], dev(dc=1)).wait_recv()
            remote(xb.at[dd, e], xb.at[dd, e], xb_s.at[k], xb_r.at[k], dev(dc=1)).wait_recv()
        for d in ds:
            sa = ta[d, 0, x].astype(F32)
            sb = tb[d, 0, i].astype(F32)
            for e in range(1, 8):
                sa = sa + xa[d, e].astype(F32)
                sb = sb + xb[d, e].astype(F32)
            dst = ys if d else yr
            dst[d, 0:24] = sa
            dst[d, 24:32] = sb
            if d:
                send(remote(ys.at[d], yr.at[d], y_s.at[d], y_r.at[d], dev(dy=STEPS[d])))

    def arrive(step, h):
        came = [direction for direction in range(2) if ag_has(direction, step, h)]
        for direction in came:
            ag(direction, step, h).wait_recv()
            if step < 4 and ag_has(direction, step + 1, h):
                send(ag(direction, step + 1, h))
        for direction in came:
            send(to_sibling(GROUPS[step][direction] if step < 4 else 7, h))

    def other(d):
        for h in range(2):
            to_sibling(d, h).wait_recv()
        tile(d, 1)

    for direction in range(2):
        send(ag(direction, 1, 0))
    tile(0, 1)
    for direction in range(2):
        send(ag(direction, 1, 1))
    terms(0, 1)
    tile(0, 0)
    terms(0, 0)
    arrive(1, 0)
    arrive(1, 1)
    for step in range(1, 4):
        low, high = GROUPS[step]
        tile(low, 0)
        arrive(step + 1, 0)
        tile(high, 0)
        terms(step, 0)
        arrive(step + 1, 1)
        other(low)
        other(high)
        terms(step, 1)
        reduce_group(step - 1)
    tile(7, 0)
    terms(4, 0)
    other(7)
    terms(4, 1)
    reduce_group(3)
    reduce_group(4)

    table = vt[...].reshape(2048, 512)
    gram = 0.05 * dot(table, table, 0, 0)
    hi = gram.astype(BF16)
    gh[0] = hi
    rest = gram - hi.astype(F32)
    mid = rest.astype(BF16)
    gh[1] = mid
    gh[2] = (rest - mid.astype(F32)).astype(BF16)

    drain(7)
    total = yr[0]
    for d in range(1, 8):
        remote(yr.at[d], yr.at[d], y_s.at[d], y_r.at[d], dev(dc=1)).wait_recv()
        total = total + yr[d]
    for n in range(4):
        qa[n] = total[0:24, 128 * n : 128 * n + 128]
        qb[n] = total[24:32, 128 * n : 128 * n + 128]
    for d in range(1, 4):
        send(remote(qa.at[lax.rem(i + d, 4)], za.at[d], z_s.at[d], z_r.at[d], dev(di=d)))
        send(remote(qb.at[lax.rem(x + d, 4)], zb.at[d], z_s.at[4 + d], z_r.at[4 + d], dev(dx=d)))

    def user(j):
        uj = uv[j]
        acc = 0.1 * uj.astype(F32)
        for n in range(3):
            acc = acc + dot(uj, gh[n], 1, 0)
        for b in range(16):
            acc = acc + dot(rm[b, j], vt[b].reshape(128, 512), 1, 0)
        ug[j] = acc

    user(0)
    user(1)

    pa, pb = qa[i], qb[x]
    for d in range(1, 4):
        remote(za.at[d], za.at[d], z_s.at[d], z_r.at[d], dev(dc=1)).wait_recv()
        remote(zb.at[d], zb.at[d], z_s.at[4 + d], z_r.at[4 + d], dev(dc=1)).wait_recv()
        pa = pa + za[d]
        pb = pb + zb[d]
    z1[0:24] = pa
    z1[24:32] = pb
    for d in range(1, 3):
        send(remote(z1, tr.at[g], z_s.at[8 + d], z_r.at[8 + d], dev(dg=d)))
    tr[g] = z1[...]
    user(2)
    user(3)
    drain(2)
    for d in range(1, 3):
        remote(z1, z1, z_s.at[8 + d], z_r.at[8 + d], dev(dc=1)).wait_recv()
    ob[c, x, i] = tr[0] + tr[1] + tr[2]

    def spread(ref, k, to):
        return remote(ref, ref, g_s.at[k], g_r.at[k], to)

    for dx in (2, 1, 3, 0):
        for di in (2, 1, 3, 0):
            if dx or di:
                send(spread(ob.at[c, x, i], dx * 4 + di, dev(dx=dx, di=di)))
    for dx in (0, 1, 3, 2):
        for di in range(4):
            if dx or di:
                spread(ob.at[c, x, i], dx * 4 + di, dev(dx=dx, di=di)).wait_recv()
        send(spread(ob.at[c, lax.rem(x + NX - dx, NX)], 16 + dx, dev(dc=1)))
    drain()
    for dx in range(NX):
        spread(ob.at[c, x], 16 + dx, dev(dc=1)).wait_recv()
    own = vt[pl.ds(2 * y, 2)].reshape(256, 512)
    for cc in range(2):
        for xx in range(NX):
            for ii in range(4):
                lo = cc * 128 + 24 * xx
                ig[lo : lo + 24, 128 * ii : 128 * ii + 128] = ob[cc, xx, ii, 0:24]
                lo = cc * 128 + 96 + 8 * ii
                ig[lo : lo + 8, 128 * xx : 128 * xx + 128] = ob[cc, xx, ii, 24:32]
    ig[...] = ig[...] * (1.0 / 32.0) + 0.1 * own.astype(F32)


def place(ug, ig, ug_out, ig_out, sem):
    cps = [pltpu.make_async_copy(ug.at[j], ug_out.at[j], sem.at[j]) for j in range(4)]
    cps.append(pltpu.make_async_copy(ig, ig_out, sem.at[4]))
    for cp in cps:
        cp.start()
    for cp in cps:
        cp.wait()


def local(user_factors, item_factors, obs_user, obs_item, obs_weight, obs_target):
    hbm = pl.BlockSpec(memory_space=pltpu.HBM)
    vmem = pl.BlockSpec(memory_space=pltpu.VMEM)
    smem = pl.BlockSpec(memory_space=pltpu.SMEM)
    dma = pltpu.SemaphoreType.DMA
    shapes = (
        jax.ShapeDtypeStruct((4, 128, 512), F32),
        jax.ShapeDtypeStruct((256, 512), F32),
    )
    made = pl.pallas_call(
        kernel,
        out_shape=tuple(pltpu.VMEM(a.shape, a.dtype) for a in shapes),
        in_specs=[smem, smem, hbm, hbm, hbm, hbm],
        out_specs=(vmem, vmem),
        scratch_shapes=[
            pltpu.VMEM((4, 128, 512), BF16),
            pltpu.VMEM((16, 2, 64, 512), BF16),
            pltpu.VMEM((8, 128, 128), BF16),
            pltpu.VMEM((8, 128, 128), BF16),
            pltpu.VMEM((8, 2, 4, 24, 512), BF16),
            pltpu.VMEM((8, 2, 4, 8, 512), BF16),
            pltpu.VMEM((8, 8, 24, 512), BF16),
            pltpu.VMEM((8, 8, 8, 512), BF16),
            pltpu.VMEM((8, 32, 512), F32),
            pltpu.VMEM((8, 32, 512), F32),
            pltpu.VMEM((4, 24, 128), F32),
            pltpu.VMEM((4, 8, 128), F32),
            pltpu.VMEM((4, 24, 128), F32),
            pltpu.VMEM((4, 8, 128), F32),
            pltpu.VMEM((32, 128), F32),
            pltpu.VMEM((3, 32, 128), F32),
            pltpu.VMEM((2, 4, 4, 32, 128), F32),
            pltpu.VMEM((16, 4, 128, 128), BF16),
            pltpu.VMEM((3, 512, 512), BF16),
            dma((4,)),
            dma((16,)), dma((16,)),
            dma((16,)), dma((16,)),
            dma((40,)), dma((40,)),
            dma((40,)), dma((40,)),
            dma((8,)), dma((8,)),
            dma((12,)), dma((12,)),
            dma((20,)), dma((20,)),
        ],
        compiler_params=pltpu.CompilerParams(
            collective_id=0, has_side_effects=True, vmem_limit_bytes=VMEM
        ),
    )(
        obs_user,
        obs_item,
        user_factors.reshape(4, 128, 512),
        item_factors.reshape(2, 2, 64, 512),
        obs_weight,
        obs_target,
    )
    user_grad, item_grad = pl.pallas_call(
        place,
        out_shape=shapes,
        in_specs=[vmem, vmem],
        out_specs=(hbm, hbm),
        scratch_shapes=[dma((5,))],
        compiler_params=pltpu.CompilerParams(vmem_limit_bytes=VMEM),
    )(*(pltpu.with_memory_space_constraint(m, pltpu.VMEM) for m in made))
    return user_grad.reshape(512, 512), item_grad


def solution(mesh):
    both = P(("rows", "grp"))
    placed = (
        P(("rows", "grp"), None),
        P("grp", None),
        both,
        both,
        P(("rows", "grp"), None, None),
        P(("rows", "grp"), None, None),
    )
    return jax.shard_map(
        local,
        mesh=mesh,
        in_specs=placed,
        out_specs=(P(("rows", "grp"), None), P("grp", None)),
        check_vma=False,
    )
```

```python
import jax
import jax.numpy as jnp
from jax import lax
from jax.experimental import pallas as pl
from jax.experimental.pallas import tpu as pltpu
from jax.sharding import PartitionSpec as P

MESH = pl.DeviceIdType.MESH
NX, NY = 4, 8
STEPS = [0, -1, 1, -2, 2, -3, 3, 4]
GROUPS = [[0], [1, 2], [3, 4], [5, 6], [7]]
VMEM = 56 << 20
FULL_BARRIER = 0
F32 = jnp.float32
BF16 = jnp.bfloat16


def dot(a, b, ca, cb):
    return lax.dot_general(a, b, (((ca,), (cb,)), ((), ())), preferred_element_type=F32)


def kernel(
    user_hbm, item_hbm, u_hbm, v_hbm, w_hbm, t_hbm, ug, ig,
    obs_user, obs_item, uv, vt, wv, tv, ta, tb, xa, xb, ys, yr, qa, qb, za, zb, z1, tr, ob, rm, gh,
    sem_in, ag_s, ag_r, sb_s, sb_r, xa_s, xa_r, xb_s, xb_r,
    y_s, y_r, z_s, z_r, g_s, g_r,
):
    r = lax.axis_index("rows")
    y = lax.axis_index("grp")
    c = lax.rem(r, 2)
    x = lax.rem(r // 2, NX)
    z = r // (2 * NX)
    i, g = lax.rem(z, 4), z // 4

    def dev(dx=0, dy=0, di=0, dg=0, dc=0):
        cc = 1 - c if dc else c
        xx = lax.rem(x + dx, NX) if dx else x
        yy = lax.rem(y + dy + NY, NY) if dy else y
        gg = lax.rem(g + dg, 3) if dg else g
        zz = gg * 4 + (lax.rem(i + di, 4) if di else i)
        return ((zz * NX + xx) * 2 + cc, yy)

    def yat(d):
        return lax.rem(y + STEPS[d] + NY, NY)

    def remote(src, dst, s, t, to):
        return pltpu.make_async_remote_copy(src, dst, s, t, device_id=to, device_id_type=MESH)

    pending = []

    def drain(keep=0):
        while len(pending) > keep:
            pending.pop(0).wait_send()

    def send(cp):
        cp.start()
        pending.append(cp)

    peers = [dev(dy=1), dev(dy=-1), dev(dc=1)]
    peers += [dev(dx=d, dc=dc) for d in range(1, 4) for dc in range(2)]
    peers += [dev(di=d, dc=dc) for d in range(1, 4) for dc in range(2)]
    peers += [dev(dg=1), dev(dg=2)]
    if FULL_BARRIER:
        peers += [dev(dy=d) for d in range(2, 7)]
        peers += [dev(dx=dx, di=di) for dx in range(1, 4) for di in range(1, 4)]
    barrier = pltpu.get_barrier_semaphore()
    for p in reversed(peers):
        pl.semaphore_signal(barrier, inc=1, device_id=p, device_id_type=MESH)
    loads = [
        pltpu.make_async_copy(v_hbm, vt.at[pl.ds(2 * y, 2)], sem_in.at[0]),
        pltpu.make_async_copy(u_hbm, uv, sem_in.at[1]),
        pltpu.make_async_copy(w_hbm, wv, sem_in.at[2]),
        pltpu.make_async_copy(t_hbm, tv, sem_in.at[3]),
        pltpu.make_async_copy(user_hbm, obs_user, sem_in.at[4]),
        pltpu.make_async_copy(item_hbm, obs_item, sem_in.at[5]),
    ]
    for cp in loads:
        cp.start()
    for cp in loads:
        cp.wait()
    pl.semaphore_wait(barrier, len(peers))

    def ag(direction, step, h):
        sgn = 1 if direction == 0 else -1
        src_y = lax.rem(y - sgn * (step - 1) + NY, NY)
        ref = vt.at[2 * src_y + c, h]
        k = (direction * 4 + step - 1) * 2 + h
        return remote(ref, ref, ag_s.at[k], ag_r.at[k], dev(dy=sgn))

    def ag_has(direction, step, h):
        return step < 4 or h == direction

    def to_sibling(d, h):
        ref = vt.at[2 * yat(d) + c, h]
        return remote(ref, ref, sb_s.at[2 * d + h], sb_r.at[2 * d + h], dev(dc=1))

    def tile(d, dc):
        yy = yat(d)
        cc = 1 - c if dc else c
        b = 2 * yy + cc
        k = jnp.int32(0)
        scale = F32(0.0)
        for n in range(8):
            hit = obs_item[n] == b
            k = jnp.where(hit, n, k)
            scale = jnp.where(hit, F32(0.0625), scale)
        j = obs_user[k]
        uk = uv[j]
        vb = vt[b].reshape(128, 512)
        predicted = dot(uk, vb, 1, 1)
        res = (wv[k].astype(F32) * (predicted - tv[k].astype(F32)) * scale).astype(BF16)
        term = dot(res, uk, 0, 0)
        for n in range(4):
            ta[d, dc, n] = term[24 * n : 24 * n + 24].astype(BF16)
            tb[d, dc, n] = term[96 + 8 * n : 104 + 8 * n].astype(BF16)
        for jj in range(4):
            keep = jnp.where(j == jj, F32(1.0), F32(0.0)).astype(BF16)
            rm[b, jj] = res * keep

    def terms(grp, dc):
        ds = GROUPS[grp]
        dd = pl.ds(ds[0], len(ds))
        for n in (2, 1, 3, 0):
            if n or dc:
                e = n * 2 + dc
                k = grp * 8 + e
                xx = lax.rem(x + n, NX)
                ii = lax.rem(i + n, 4)
                send(remote(ta.at[dd, dc, xx], xa.at[dd, e], xa_s.at[k], xa_r.at[k], dev(dx=n, dc=dc)))
                send(remote(tb.at[dd, dc, ii], xb.at[dd, e], xb_s.at[k], xb_r.at[k], dev(di=n, dc=dc)))

    def reduce_group(grp):
        ds = GROUPS[grp]
        dd = pl.ds(ds[0], len(ds))
        for e in range(1, 8):
            k = grp * 8 + e
            remote(xa.at[dd, e], xa.at[dd, e], xa_s.at[k], xa_r.at[k], dev(dc=1)).wait_recv()
            remote(xb.at[dd, e], xb.at[dd, e], xb_s.at[k], xb_r.at[k], dev(dc=1)).wait_recv()
        for d in ds:
            sa = ta[d, 0, x].astype(F32)
            sb = tb[d, 0, i].astype(F32)
            for e in range(1, 8):
                sa = sa + xa[d, e].astype(F32)
                sb = sb + xb[d, e].astype(F32)
            dst = ys if d else yr
            dst[d, 0:24] = sa
            dst[d, 24:32] = sb
            if d:
                send(remote(ys.at[d], yr.at[d], y_s.at[d], y_r.at[d], dev(dy=STEPS[d])))

    def arrive(step, h):
        came = [direction for direction in range(2) if ag_has(direction, step, h)]
        for direction in came:
            ag(direction, step, h).wait_recv()
            if step < 4 and ag_has(direction, step + 1, h):
                send(ag(direction, step + 1, h))
        for direction in came:
            send(to_sibling(GROUPS[step][direction] if step < 4 else 7, h))

    def other(d):
        for h in range(2):
            to_sibling(d, h).wait_recv()
        tile(d, 1)

    for h in range(2):
        for direction in range(2):
            send(ag(direction, 1, h))
    tile(0, 1)
    terms(0, 1)
    tile(0, 0)
    terms(0, 0)
    arrive(1, 0)
    arrive(1, 1)
    for step in range(1, 4):
        low, high = GROUPS[step]
        tile(low, 0)
        arrive(step + 1, 0)
        tile(high, 0)
        terms(step, 0)
        arrive(step + 1, 1)
        other(low)
        other(high)
        terms(step, 1)
        reduce_group(step - 1)
    tile(7, 0)
    terms(4, 0)
    other(7)
    terms(4, 1)
    reduce_group(3)
    reduce_group(4)

    table = vt[...].reshape(2048, 512)
    gram = 0.05 * dot(table, table, 0, 0)
    hi = gram.astype(BF16)
    gh[0] = hi
    rest = gram - hi.astype(F32)
    mid = rest.astype(BF16)
    gh[1] = mid
    gh[2] = (rest - mid.astype(F32)).astype(BF16)

    drain(7)
    total = yr[0]
    for d in range(1, 8):
        remote(yr.at[d], yr.at[d], y_s.at[d], y_r.at[d], dev(dc=1)).wait_recv()
        total = total + yr[d]
    for n in range(4):
        qa[n] = total[0:24, 128 * n : 128 * n + 128]
        qb[n] = total[24:32, 128 * n : 128 * n + 128]
    for d in range(1, 4):
        send(remote(qa.at[lax.rem(i + d, 4)], za.at[d], z_s.at[d], z_r.at[d], dev(di=d)))
        send(remote(qb.at[lax.rem(x + d, 4)], zb.at[d], z_s.at[4 + d], z_r.at[4 + d], dev(dx=d)))

    def user(j):
        uj = uv[j]
        acc = 0.1 * uj.astype(F32)
        for n in range(3):
            acc = acc + dot(uj, gh[n], 1, 0)
        for b in range(16):
            acc = acc + dot(rm[b, j], vt[b].reshape(128, 512), 1, 0)
        ug[j] = acc

    user(0)
    user(1)

    pa, pb = qa[i], qb[x]
    for d in range(1, 4):
        remote(za.at[d], za.at[d], z_s.at[d], z_r.at[d], dev(dc=1)).wait_recv()
        remote(zb.at[d], zb.at[d], z_s.at[4 + d], z_r.at[4 + d], dev(dc=1)).wait_recv()
        pa = pa + za[d]
        pb = pb + zb[d]
    z1[0:24] = pa
    z1[24:32] = pb
    for d in range(1, 3):
        send(remote(z1, tr.at[g], z_s.at[8 + d], z_r.at[8 + d], dev(dg=d)))
    tr[g] = z1[...]
    user(2)
    user(3)
    drain(2)
    for d in range(1, 3):
        remote(z1, z1, z_s.at[8 + d], z_r.at[8 + d], dev(dc=1)).wait_recv()
    ob[c, x, i] = tr[0] + tr[1] + tr[2]

    def spread(ref, k, to):
        return remote(ref, ref, g_s.at[k], g_r.at[k], to)

    for dx in (2, 1, 3, 0):
        for di in (2, 1, 3, 0):
            if dx or di:
                send(spread(ob.at[c, x, i], dx * 4 + di, dev(dx=dx, di=di)))
    for dx in (0, 1, 3, 2):
        for di in range(4):
            if dx or di:
                spread(ob.at[c, x, i], dx * 4 + di, dev(dx=dx, di=di)).wait_recv()
        send(spread(ob.at[c, lax.rem(x + NX - dx, NX)], 16 + dx, dev(dc=1)))
    drain()
    for dx in range(NX):
        spread(ob.at[c, x], 16 + dx, dev(dc=1)).wait_recv()
    own = vt[pl.ds(2 * y, 2)].reshape(256, 512)
    for cc in range(2):
        for xx in range(NX):
            for ii in range(4):
                lo = cc * 128 + 24 * xx
                ig[lo : lo + 24, 128 * ii : 128 * ii + 128] = ob[cc, xx, ii, 0:24]
                lo = cc * 128 + 96 + 8 * ii
                ig[lo : lo + 8, 128 * xx : 128 * xx + 128] = ob[cc, xx, ii, 24:32]
    ig[...] = ig[...] * (1.0 / 32.0) + 0.1 * own.astype(F32)


def place(ug, ig, ug_out, ig_out, sem):
    cps = [pltpu.make_async_copy(ug.at[j], ug_out.at[j], sem.at[j]) for j in range(4)]
    cps.append(pltpu.make_async_copy(ig, ig_out, sem.at[4]))
    for cp in cps:
        cp.start()
    for cp in cps:
        cp.wait()


def local(user_factors, item_factors, obs_user, obs_item, obs_weight, obs_target):
    hbm = pl.BlockSpec(memory_space=pltpu.HBM)
    vmem = pl.BlockSpec(memory_space=pltpu.VMEM)
    dma = pltpu.SemaphoreType.DMA
    shapes = (
        jax.ShapeDtypeStruct((4, 128, 512), F32),
        jax.ShapeDtypeStruct((256, 512), F32),
    )
    made = pl.pallas_call(
        kernel,
        out_shape=tuple(pltpu.VMEM(a.shape, a.dtype) for a in shapes),
        in_specs=[hbm, hbm, hbm, hbm, hbm, hbm],
        out_specs=(vmem, vmem),
        scratch_shapes=[
            pltpu.SMEM((8,), jnp.int32),
            pltpu.SMEM((8,), jnp.int32),
            pltpu.VMEM((4, 128, 512), BF16),
            pltpu.VMEM((16, 2, 64, 512), BF16),
            pltpu.VMEM((8, 128, 128), BF16),
            pltpu.VMEM((8, 128, 128), BF16),
            pltpu.VMEM((8, 2, 4, 24, 512), BF16),
            pltpu.VMEM((8, 2, 4, 8, 512), BF16),
            pltpu.VMEM((8, 8, 24, 512), BF16),
            pltpu.VMEM((8, 8, 8, 512), BF16),
            pltpu.VMEM((8, 32, 512), F32),
            pltpu.VMEM((8, 32, 512), F32),
            pltpu.VMEM((4, 24, 128), F32),
            pltpu.VMEM((4, 8, 128), F32),
            pltpu.VMEM((4, 24, 128), F32),
            pltpu.VMEM((4, 8, 128), F32),
            pltpu.VMEM((32, 128), F32),
            pltpu.VMEM((3, 32, 128), F32),
            pltpu.VMEM((2, 4, 4, 32, 128), F32),
            pltpu.VMEM((16, 4, 128, 128), BF16),
            pltpu.VMEM((3, 512, 512), BF16),
            dma((6,)),
            dma((16,)), dma((16,)),
            dma((16,)), dma((16,)),
            dma((40,)), dma((40,)),
            dma((40,)), dma((40,)),
            dma((8,)), dma((8,)),
            dma((12,)), dma((12,)),
            dma((20,)), dma((20,)),
        ],
        compiler_params=pltpu.CompilerParams(
            collective_id=0, has_side_effects=True, vmem_limit_bytes=VMEM
        ),
    )(
        obs_user,
        obs_item,
        user_factors.reshape(4, 128, 512),
        item_factors.reshape(2, 2, 64, 512),
        obs_weight,
        obs_target,
    )
    user_grad, item_grad = pl.pallas_call(
        place,
        out_shape=shapes,
        in_specs=[vmem, vmem],
        out_specs=(hbm, hbm),
        scratch_shapes=[dma((5,))],
        compiler_params=pltpu.CompilerParams(vmem_limit_bytes=VMEM),
    )(*(pltpu.with_memory_space_constraint(m, pltpu.VMEM) for m in made))
    return user_grad.reshape(512, 512), item_grad


def solution(mesh):
    both = P(("rows", "grp"))
    placed = (
        P(("rows", "grp"), None),
        P("grp", None),
        both,
        both,
        P(("rows", "grp"), None, None),
        P(("rows", "grp"), None, None),
    )
    return jax.shard_map(
        local,
        mesh=mesh,
        in_specs=placed,
        out_specs=(P(("rows", "grp"), None), P("grp", None)),
        check_vma=False,
    )
```

```python
import jax
import jax.numpy as jnp
from jax import lax
from jax.experimental import pallas as pl
from jax.experimental.pallas import tpu as pltpu
from jax.sharding import PartitionSpec as P

MESH = pl.DeviceIdType.MESH
NX, NY = 4, 8
STEPS = [0, -1, 1, -2, 2, -3, 3, 4]
GROUPS = [[0], [1, 2], [3, 4], [5, 6], [7]]
VMEM = 56 << 20
FULL_BARRIER = 0
F32 = jnp.float32
BF16 = jnp.bfloat16


def dot(a, b, ca, cb):
    return lax.dot_general(a, b, (((ca,), (cb,)), ((), ())), preferred_element_type=F32)


def kernel(
    user_hbm, item_hbm, u_hbm, v_hbm, w_hbm, t_hbm, ug, ig,
    obs_user, obs_item, uv, vt, wv, tv, ta, tb, xa, xb, ys, yr, qa, qb, za, zb, z1, tr, ob, rm, gh,
    sem_in, ag_s, ag_r, sb_s, sb_r, xa_s, xa_r, xb_s, xb_r,
    y_s, y_r, z_s, z_r, g_s, g_r,
):
    r = lax.axis_index("rows")
    y = lax.axis_index("grp")
    c = lax.rem(r, 2)
    x = lax.rem(r // 2, NX)
    z = r // (2 * NX)
    i, g = lax.rem(z, 4), z // 4

    def dev(dx=0, dy=0, di=0, dg=0, dc=0):
        cc = 1 - c if dc else c
        xx = lax.rem(x + dx, NX) if dx else x
        yy = lax.rem(y + dy + NY, NY) if dy else y
        gg = lax.rem(g + dg, 3) if dg else g
        zz = gg * 4 + (lax.rem(i + di, 4) if di else i)
        return ((zz * NX + xx) * 2 + cc, yy)

    def yat(d):
        return lax.rem(y + STEPS[d] + NY, NY)

    def remote(src, dst, s, t, to):
        return pltpu.make_async_remote_copy(src, dst, s, t, device_id=to, device_id_type=MESH)

    pending = []

    def drain(keep=0):
        while len(pending) > keep:
            pending.pop(0).wait_send()

    def send(cp):
        cp.start()
        pending.append(cp)

    peers = [dev(dy=1), dev(dy=-1), dev(dc=1)]
    peers += [dev(dx=d, dc=dc) for d in range(1, 4) for dc in range(2)]
    peers += [dev(di=d, dc=dc) for d in range(1, 4) for dc in range(2)]
    peers += [dev(dg=1), dev(dg=2)]
    if FULL_BARRIER:
        peers += [dev(dy=d) for d in range(2, 7)]
        peers += [dev(dx=dx, di=di) for dx in range(1, 4) for di in range(1, 4)]
    barrier = pltpu.get_barrier_semaphore()
    for p in reversed(peers):
        pl.semaphore_signal(barrier, inc=1, device_id=p, device_id_type=MESH)
    loads = [
        pltpu.make_async_copy(v_hbm, vt.at[pl.ds(2 * y, 2)], sem_in.at[0]),
        pltpu.make_async_copy(u_hbm, uv, sem_in.at[1]),
        pltpu.make_async_copy(w_hbm, wv, sem_in.at[2]),
        pltpu.make_async_copy(t_hbm, tv, sem_in.at[3]),
        pltpu.make_async_copy(user_hbm, obs_user, sem_in.at[4]),
        pltpu.make_async_copy(item_hbm, obs_item, sem_in.at[5]),
    ]
    for cp in loads:
        cp.start()
    for cp in loads:
        cp.wait()
    pl.semaphore_wait(barrier, len(peers))

    def ag(direction, step, h):
        sgn = 1 if direction == 0 else -1
        src_y = lax.rem(y - sgn * (step - 1) + NY, NY)
        ref = vt.at[2 * src_y + c, h]
        k = (direction * 4 + step - 1) * 2 + h
        return remote(ref, ref, ag_s.at[k], ag_r.at[k], dev(dy=sgn))

    def ag_has(direction, step, h):
        return step < 4 or h == direction

    def to_sibling(d, h):
        ref = vt.at[2 * yat(d) + c, h]
        return remote(ref, ref, sb_s.at[2 * d + h], sb_r.at[2 * d + h], dev(dc=1))

    def tile(d, dc):
        yy = yat(d)
        cc = 1 - c if dc else c
        b = 2 * yy + cc
        k = jnp.int32(0)
        scale = F32(0.0)
        for n in range(8):
            hit = obs_item[n] == b
            k = jnp.where(hit, n, k)
            scale = jnp.where(hit, F32(0.0625), scale)
        j = obs_user[k]
        uk = uv[j]
        vb = vt[b].reshape(128, 512)
        predicted = dot(uk, vb, 1, 1)
        res = (wv[k].astype(F32) * (predicted - tv[k].astype(F32)) * scale).astype(BF16)
        term = dot(res, uk, 0, 0)
        for n in range(4):
            ta[d, dc, n] = term[24 * n : 24 * n + 24].astype(BF16)
            tb[d, dc, n] = term[96 + 8 * n : 104 + 8 * n].astype(BF16)
        for jj in range(4):
            keep = jnp.where(j == jj, F32(1.0), F32(0.0)).astype(BF16)
            rm[b, jj] = res * keep

    def terms(grp, dc):
        ds = GROUPS[grp]
        dd = pl.ds(ds[0], len(ds))
        for n in (2, 1, 3, 0):
            if n or dc:
                e = n * 2 + dc
                k = grp * 8 + e
                xx = lax.rem(x + n, NX)
                ii = lax.rem(i + n, 4)
                send(remote(ta.at[dd, dc, xx], xa.at[dd, e], xa_s.at[k], xa_r.at[k], dev(dx=n, dc=dc)))
                send(remote(tb.at[dd, dc, ii], xb.at[dd, e], xb_s.at[k], xb_r.at[k], dev(di=n, dc=dc)))

    def reduce_group(grp):
        ds = GROUPS[grp]
        dd = pl.ds(ds[0], len(ds))
        for e in range(1, 8):
            k = grp * 8 + e
            remote(xa.at[dd, e], xa.at[dd, e], xa_s.at[k], xa_r.at[k], dev(dc=1)).wait_recv()
            remote(xb.at[dd, e], xb.at[dd, e], xb_s.at[k], xb_r.at[k], dev(dc=1)).wait_recv()
        for d in ds:
            sa = ta[d, 0, x].astype(F32)
            sb = tb[d, 0, i].astype(F32)
            for e in range(1, 8):
                sa = sa + xa[d, e].astype(F32)
                sb = sb + xb[d, e].astype(F32)
            dst = ys if d else yr
            dst[d, 0:24] = sa
            dst[d, 24:32] = sb
            if d:
                send(remote(ys.at[d], yr.at[d], y_s.at[d], y_r.at[d], dev(dy=STEPS[d])))

    def arrive(step, h):
        came = [direction for direction in range(2) if ag_has(direction, step, h)]
        for direction in came:
            ag(direction, step, h).wait_recv()
            if step < 4 and ag_has(direction, step + 1, h):
                send(ag(direction, step + 1, h))
        for direction in came:
            send(to_sibling(GROUPS[step][direction] if step < 4 else 7, h))

    def other(d):
        for h in range(2):
            to_sibling(d, h).wait_recv()
        tile(d, 1)

    for h in range(2):
        for direction in range(2):
            send(ag(direction, 1, h))
    tile(0, 1)
    terms(0, 1)
    tile(0, 0)
    terms(0, 0)
    arrive(1, 0)
    arrive(1, 1)
    for step in range(1, 4):
        low, high = GROUPS[step]
        tile(low, 0)
        arrive(step + 1, 0)
        tile(high, 0)
        terms(step, 0)
        arrive(step + 1, 1)
        other(low)
        other(high)
        terms(step, 1)
        reduce_group(step - 1)
    tile(7, 0)
    terms(4, 0)
    other(7)
    terms(4, 1)
    reduce_group(3)
    reduce_group(4)

    table = vt[...].reshape(2048, 512)
    gram = 0.05 * dot(table, table, 0, 0)
    hi = gram.astype(BF16)
    gh[0] = hi
    rest = gram - hi.astype(F32)
    mid = rest.astype(BF16)
    gh[1] = mid
    gh[2] = (rest - mid.astype(F32)).astype(BF16)

    drain(7)
    total = yr[0]
    for d in range(1, 8):
        remote(yr.at[d], yr.at[d], y_s.at[d], y_r.at[d], dev(dc=1)).wait_recv()
        total = total + yr[d]
    for n in range(4):
        qa[n] = total[0:24, 128 * n : 128 * n + 128]
        qb[n] = total[24:32, 128 * n : 128 * n + 128]
    for d in range(1, 4):
        send(remote(qa.at[lax.rem(i + d, 4)], za.at[d], z_s.at[d], z_r.at[d], dev(di=d)))
        send(remote(qb.at[lax.rem(x + d, 4)], zb.at[d], z_s.at[4 + d], z_r.at[4 + d], dev(dx=d)))

    def user(j):
        uj = uv[j]
        acc = 0.1 * uj.astype(F32)
        for n in range(3):
            acc = acc + dot(uj, gh[n], 1, 0)
        for b in range(16):
            acc = acc + dot(rm[b, j], vt[b].reshape(128, 512), 1, 0)
        ug[j] = acc

    user(0)
    user(1)

    pa, pb = qa[i], qb[x]
    for d in range(1, 4):
        remote(za.at[d], za.at[d], z_s.at[d], z_r.at[d], dev(dc=1)).wait_recv()
        remote(zb.at[d], zb.at[d], z_s.at[4 + d], z_r.at[4 + d], dev(dc=1)).wait_recv()
        pa = pa + za[d]
        pb = pb + zb[d]
    z1[0:24] = pa
    z1[24:32] = pb
    for d in range(1, 3):
        send(remote(z1, tr.at[g], z_s.at[8 + d], z_r.at[8 + d], dev(dg=d)))
    tr[g] = z1[...]
    user(2)
    user(3)
    drain(2)
    for d in range(1, 3):
        remote(z1, z1, z_s.at[8 + d], z_r.at[8 + d], dev(dc=1)).wait_recv()
    ob[c, x, i] = tr[0] + tr[1] + tr[2]

    def spread(ref, k, to):
        return remote(ref, ref, g_s.at[k], g_r.at[k], to)

    for dx in (2, 1, 3, 0):
        for di in (2, 1, 3, 0):
            if dx or di:
                send(spread(ob.at[c, x, i], dx * 4 + di, dev(dx=dx, di=di)))
    own = vt[pl.ds(2 * y, 2)].reshape(256, 512)
    ig[...] = 0.1 * own.astype(F32)
    for dx in (0, 1, 3, 2):
        for di in range(4):
            if dx or di:
                spread(ob.at[c, x, i], dx * 4 + di, dev(dx=dx, di=di)).wait_recv()
        send(spread(ob.at[c, lax.rem(x + NX - dx, NX)], 16 + dx, dev(dc=1)))
    half = pl.multiple_of(c * 128, 128)

    def settle(cc, start):
        for xx in range(NX):
            for ii in range(4):
                cols = slice(128 * ii, 128 * ii + 128)
                rows = pl.ds(pl.multiple_of(start + 24 * xx, 8), 24)
                ig[rows, cols] = ig[rows, cols] + ob[cc, xx, ii, 0:24] * (1.0 / 32.0)
                cols = slice(128 * xx, 128 * xx + 128)
                rows = pl.ds(pl.multiple_of(start + 96 + 8 * ii, 8), 8)
                ig[rows, cols] = ig[rows, cols] + ob[cc, xx, ii, 24:32] * (1.0 / 32.0)

    settle(c, half)
    drain()
    for dx in range(NX):
        spread(ob.at[c, x], 16 + dx, dev(dc=1)).wait_recv()
    settle(1 - c, pl.multiple_of(128 - c * 128, 128))


def place(ug, ig, ug_out, ig_out, sem):
    cps = [pltpu.make_async_copy(ug.at[j], ug_out.at[j], sem.at[j]) for j in range(4)]
    cps.append(pltpu.make_async_copy(ig, ig_out, sem.at[4]))
    for cp in cps:
        cp.start()
    for cp in cps:
        cp.wait()


def local(user_factors, item_factors, obs_user, obs_item, obs_weight, obs_target):
    hbm = pl.BlockSpec(memory_space=pltpu.HBM)
    vmem = pl.BlockSpec(memory_space=pltpu.VMEM)
    dma = pltpu.SemaphoreType.DMA
    shapes = (
        jax.ShapeDtypeStruct((4, 128, 512), F32),
        jax.ShapeDtypeStruct((256, 512), F32),
    )
    made = pl.pallas_call(
        kernel,
        out_shape=tuple(pltpu.VMEM(a.shape, a.dtype) for a in shapes),
        in_specs=[hbm, hbm, hbm, hbm, hbm, hbm],
        out_specs=(vmem, vmem),
        scratch_shapes=[
            pltpu.SMEM((8,), jnp.int32),
            pltpu.SMEM((8,), jnp.int32),
            pltpu.VMEM((4, 128, 512), BF16),
            pltpu.VMEM((16, 2, 64, 512), BF16),
            pltpu.VMEM((8, 128, 128), BF16),
            pltpu.VMEM((8, 128, 128), BF16),
            pltpu.VMEM((8, 2, 4, 24, 512), BF16),
            pltpu.VMEM((8, 2, 4, 8, 512), BF16),
            pltpu.VMEM((8, 8, 24, 512), BF16),
            pltpu.VMEM((8, 8, 8, 512), BF16),
            pltpu.VMEM((8, 32, 512), F32),
            pltpu.VMEM((8, 32, 512), F32),
            pltpu.VMEM((4, 24, 128), F32),
            pltpu.VMEM((4, 8, 128), F32),
            pltpu.VMEM((4, 24, 128), F32),
            pltpu.VMEM((4, 8, 128), F32),
            pltpu.VMEM((32, 128), F32),
            pltpu.VMEM((3, 32, 128), F32),
            pltpu.VMEM((2, 4, 4, 32, 128), F32),
            pltpu.VMEM((16, 4, 128, 128), BF16),
            pltpu.VMEM((3, 512, 512), BF16),
            dma((6,)),
            dma((16,)), dma((16,)),
            dma((16,)), dma((16,)),
            dma((40,)), dma((40,)),
            dma((40,)), dma((40,)),
            dma((8,)), dma((8,)),
            dma((12,)), dma((12,)),
            dma((20,)), dma((20,)),
        ],
        compiler_params=pltpu.CompilerParams(
            collective_id=0, has_side_effects=True, vmem_limit_bytes=VMEM
        ),
    )(
        obs_user,
        obs_item,
        user_factors.reshape(4, 128, 512),
        item_factors.reshape(2, 2, 64, 512),
        obs_weight,
        obs_target,
    )
    user_grad, item_grad = pl.pallas_call(
        place,
        out_shape=shapes,
        in_specs=[vmem, vmem],
        out_specs=(hbm, hbm),
        scratch_shapes=[dma((5,))],
        compiler_params=pltpu.CompilerParams(vmem_limit_bytes=VMEM),
    )(*(pltpu.with_memory_space_constraint(m, pltpu.VMEM) for m in made))
    return user_grad.reshape(512, 512), item_grad


def solution(mesh):
    both = P(("rows", "grp"))
    placed = (
        P(("rows", "grp"), None),
        P("grp", None),
        both,
        both,
        P(("rows", "grp"), None, None),
        P(("rows", "grp"), None, None),
    )
    return jax.shard_map(
        local,
        mesh=mesh,
        in_specs=placed,
        out_specs=(P(("rows", "grp"), None), P("grp", None)),
        check_vma=False,
    )
```
